1024 devices in a mesh: grp: 8 (over z), exp: 16 (over y, core), rep: 8 (over x).
Axes of the slice: x: 8, y: 8, z: 8, core: 2. Of those that a mesh axis runs over, the one named last changes fastest.
Arguments:
- tokens: bfloat16 [16384, 2048], P(('rep', 'grp', 'exp')), parts along dimension 0, may hold values from -6 to 6
- expert_ids: int32 [16384, 8], P(('rep', 'grp', 'exp')), parts along dimension 0, may hold values from 0 to 127, as said below
- gate_weights: bfloat16 [16384, 8], P(('rep', 'grp', 'exp')), parts along dimension 0, may hold values from 0.049804688 to 0.3984375
- w_gate: bfloat16 [128, 2048, 768], P(('grp', 'exp')), may hold values from -0.125 to 0.125
- w_up: bfloat16 [128, 2048, 768], P(('grp', 'exp')), may hold values from -0.125 to 0.125
- w_down: bfloat16 [128, 768, 2048], P(('grp', 'exp')), may hold values from -0.21875 to 0.21875
Outputs:
- combined: float32 [16384, 2048], P(('rep', 'grp', 'exp')), parts along dimension 0
The draws below stay inside these ranges and needn't reach their ends.
There are 8 independent parts, one for each index of `rep`. The reference program is written for one: setup_inputs(seed, part) draws one part's arguments, and reference() takes and returns one part's arrays. A program takes and returns all parts, laid end to end along the dimension named above; an argument that names none is the same for every part. Nothing has to cross between parts.
Inputs may be any that keep to these rules, and one draw needn't show every extreme that they name: `expert_ids`: expert x belongs to group x // 16. Each row names 8 different experts, 4 of them in each of two different groups. Of the 16 rows of one device (aligned blocks of 16 rows), at most 8 name experts of any one group and at most 2 name any one expert; in every draw one group is named by 8 rows of every device, and each of its experts by 2 rows of every device.
All inputs are finite; a program needn't handle non-finite values.
Results may differ from the reference program's by a relative error of at most 0.0041.
Values may be sent and summed in bfloat16 or wider, within the bound.
A program may use at most 32 MiB of HBM per device.

```python
from functools import partial
import jax
import jax.numpy as jnp
from jax import lax

D = 2048
FF = 768
TOP = 8
PER_GROUP = 4
TOK_DEV = 16
GROUPS = 8
GRP_EXPERTS = 16
EXPERTS = 128
TOKENS = 2048
CAP_GRP = 8
CAP_EXP = 2


def pick_index(pick_key, eligible):
    priority = jax.random.randint(pick_key, eligible.shape, 0, 1 << 20)
    return jnp.argmax(jnp.where(eligible, priority, -1)).astype(jnp.int32)


def shuffle_row(row_key, id_row):
    return jax.random.permutation(row_key, id_row)


def group_order(group_key):
    return jax.random.permutation(group_key, GRP_EXPERTS)


def device_routes(device_key, busiest):
    mean_load = 2 * TOK_DEV // GROUPS
    group_grid = jnp.arange(GROUPS, dtype=jnp.int32)
    counts = jnp.full((GROUPS,), mean_load, jnp.int32).at[busiest].set(CAP_GRP)

    def lower_one(step_index, counts):
        eligible = (counts > 0) & (group_grid != busiest)
        chosen = pick_index(jax.random.fold_in(device_key, step_index), eligible)
        return counts.at[chosen].add(-1)
    counts = lax.fori_loop(0, CAP_GRP - mean_load, lower_one, counts)

    def shuffle(step_index, counts):
        source = pick_index(jax.random.fold_in(device_key, 1000 + step_index), (counts > 0) & (group_grid != busiest))
        target = pick_index(jax.random.fold_in(device_key, 5000 + step_index), (counts < CAP_GRP - 1) & (group_grid != busiest) & (group_grid != source))
        shifted = counts.at[source].add(-1).at[target].add(1)
        allowed = (counts[source] > 0) & (counts[target] < CAP_GRP - 1) & (source != target) & (source != busiest) & (target != busiest)
        return jnp.where(allowed, shifted, counts)
    counts = lax.fori_loop(0, 2 * GROUPS, shuffle, counts)
    run_ends = jnp.cumsum(counts)
    starts = run_ends - counts
    positions = jnp.arange(2 * TOK_DEV, dtype=jnp.int32)
    labels = jnp.sum((run_ends[None, :] <= positions[:, None]).astype(jnp.int32), axis=1)
    rank_in_group = positions - starts[labels]
    orders = jax.vmap(group_order)(jax.random.split(jax.random.fold_in(device_key, 9000), GROUPS))
    spot_index = PER_GROUP * rank_in_group[:, None] + jnp.arange(PER_GROUP, dtype=jnp.int32)[None, :]
    local_ids = orders[labels[:, None], spot_index % GRP_EXPERTS]
    chosen_ids = labels[:, None] * GRP_EXPERTS + local_ids
    id_rows = jnp.concatenate([chosen_ids[:TOK_DEV], chosen_ids[TOK_DEV:]], axis=1)
    id_rows = jax.vmap(shuffle_row)(jax.random.split(jax.random.fold_in(device_key, 9100), TOK_DEV), id_rows)
    id_rows = jax.random.permutation(jax.random.fold_in(device_key, 9200), id_rows, axis=0)
    return id_rows.astype(jnp.int32)


def draw_expert_ids(key, part):
    busiest = jax.random.randint(jax.random.fold_in(key, 7), (), 0, GROUPS).astype(jnp.int32)
    device_keys = jax.random.split(jax.random.fold_in(key, 8), GROUPS * GRP_EXPERTS)
    all_devices = jax.vmap(partial(device_routes, busiest=busiest))(device_keys)
    return all_devices.reshape(TOKENS, TOP)


def levels(own_key, shape, cuts, low, largest):
    factor_of, own = 1.0, jax.random.fold_in(own_key, 6)
    for dim, parts in cuts:
        heights = jnp.exp(jax.random.uniform(jax.random.fold_in(own, dim), (parts,), jnp.float32, low / len(cuts), largest / len(cuts)))
        factor_of = factor_of * jnp.repeat(heights, shape[dim] // parts).reshape([-1 if axis == dim else 1 for axis in range(len(shape))])
    return factor_of


def gaussian(key, shape, scale, bound, cuts=(), kind=jnp.bfloat16):
    result = scale * jax.random.normal(key, shape, jnp.float32)
    if cuts:
        result = result * levels(key, shape, cuts, -0.22, 0.18)
    return jnp.clip(result, -bound, bound).astype(kind)


def setup_inputs(seed: int = 0, part: int = 0) -> dict:
    seeds = jax.random.split(jax.random.key(seed), 7)
    own_keys = jax.random.split(jax.random.fold_in(seeds[6], part), 7)
    return {
        "tokens": gaussian(own_keys[0], (TOKENS, D), 1.0, 6.0, ((0, 128),)),
        "expert_ids": draw_expert_ids(jax.random.fold_in(jax.random.fold_in(seeds[6], part), 71), part),
        "gate_weights": jnp.clip(0.049804688 + 0.3486328 * jax.random.uniform(own_keys[2], (TOKENS, TOP), jnp.float32) ** levels(own_keys[2], (TOKENS, TOP), ((0, 128),), -0.2, 0.2), 0.049804688, 0.3984375).astype(jnp.bfloat16),
        "w_gate": gaussian(seeds[3], (EXPERTS, D, FF), D ** -0.5, 0.125, ((0, 128),)),
        "w_up": gaussian(seeds[4], (EXPERTS, D, FF), D ** -0.5, 0.125, ((0, 128),)),
        "w_down": gaussian(seeds[5], (EXPERTS, FF, D), FF ** -0.5, 0.21875, ((0, 128),)),
    }


def expert_apply(token_rows, gate_mat, up_mat, down_mat):
    gate_pre = jnp.dot(token_rows, gate_mat, preferred_element_type=jnp.float32)
    up_pre = jnp.dot(token_rows, up_mat, preferred_element_type=jnp.float32)
    hidden = (jax.nn.silu(gate_pre) * up_pre).astype(jnp.bfloat16)
    return jnp.dot(hidden, down_mat, preferred_element_type=jnp.float32).astype(jnp.bfloat16)


def reference(tokens, expert_ids, gate_weights, w_gate, w_up, w_down):
    flat_ids = expert_ids.reshape(-1)
    flat_gates = gate_weights.reshape(-1).astype(jnp.float32)
    capacity = GROUPS * GRP_EXPERTS * CAP_EXP

    def visit_expert(running, expert):
        chosen = flat_ids == expert
        ordering = jnp.argsort(jnp.where(chosen, 0, 1).astype(jnp.int32), stable=True)[:capacity]
        row_index = (ordering // TOP).astype(jnp.int32)
        outputs = expert_apply(tokens[row_index], w_gate[expert], w_up[expert], w_down[expert])
        weights = jnp.where(chosen[ordering], flat_gates[ordering], jnp.zeros((), jnp.float32))
        running = running.at[row_index].add(weights[:, None] * outputs.astype(jnp.float32))
        return running, None

    running, unused = lax.scan(visit_expert, jnp.zeros((TOKENS, D), jnp.float32), jnp.arange(EXPERTS, dtype=jnp.int32))
    return running
```

```python
import functools
import jax
import jax.numpy as jnp
from jax import lax
from jax.experimental import pallas as pl
from jax.experimental.pallas import tpu as pltpu
from jax.sharding import PartitionSpec as P

F32 = jnp.float32
BF16 = jnp.bfloat16
STREAMS = 4
TILE = 256


def iota(shape, dim):
    return lax.broadcasted_iota(jnp.int32, shape, dim)


def dot(a, b):
    return jnp.dot(a, b, preferred_element_type=F32)


def dot_nt(a, b):
    return lax.dot_general(a, b, (((1,), (1,)), ((), ())), preferred_element_type=F32)


def kernel(
    ring,
    ids_ref, gates_ref, tok_ref, wg_hbm, wu_hbm, wd_hbm, o_ref,
    g_own, g_in, c_tab, s_tab, in1, out2, in2, out3, in3, out4, in4,
    wg, wu, wd, acc_g, acc_u, hid,
    w_sem, g_send, g_recv, send1, recv1, send2, recv2, send3, recv3, send4, recv4,
):
    toks, width = tok_ref.shape
    ff = wg.shape[1]
    blocks = 2 * ring
    rows2 = blocks * blocks
    rows1 = ring * toks
    experts = ring * blocks
    cols = width // STREAMS
    z = lax.axis_index("grp")
    e = lax.axis_index("exp")
    y = e // 2
    c = lax.rem(e, 2)

    def path_of(s):
        return s % 2

    def near(path, d):
        if path == 0:
            other = lax.rem(z + d, ring)
            return other, {"grp": other, "exp": e}
        other = lax.rem(y + d, ring)
        return other, {"grp": z, "exp": other * 2 + c}

    def near_me(path):
        return z if path == 0 else y

    def far(path, d, f):
        core = lax.rem(c + f, 2)
        if path == 0:
            other = lax.rem(y + d, ring) * 2 + core
            return other, {"grp": z, "exp": other}
        other = lax.rem(z + d, ring)
        return other * 2 + core, {"grp": other, "exp": y * 2 + core}

    def far_me(path):
        return e if path == 0 else z * 2 + c

    def distance(j):
        return ring // 2 + ((j + 1) // 2) * (1 - 2 * lax.rem(j, 2))

    def each_near(body):
        lax.fori_loop(0, ring - 1, lambda j, x: (body(distance(j)), x)[1], 0)

    def each_far(body):
        lax.fori_loop(
            0, 2 * (ring - 1), lambda j, x: (body(distance(j // 2), lax.rem(j, 2)), x)[1], 0
        )
        body(0, 1)

    def remote(src, dst, send, recv, device):
        return pltpu.make_async_remote_copy(
            src_ref=src, dst_ref=dst, send_sem=send, recv_sem=recv,
            device_id=device, device_id_type=pl.DeviceIdType.MESH,
        )

    def wait_bytes(ref, count, sem):
        part = ref.at[pl.ds(0, count)]
        pltpu.make_async_copy(part, part, sem).wait()

    loads = [
        pltpu.make_async_copy(hbm, vmem, w_sem.at[i])
        for i, (hbm, vmem) in enumerate(((wg_hbm, wg), (wu_hbm, wu), (wd_hbm, wd)))
    ]
    for load in loads:
        load.start()

    barrier = pltpu.get_barrier_semaphore()

    for path in range(2):
        def greet(d, f, path=path):
            pl.semaphore_signal(
                barrier, inc=1, device_id=far(path, d, f)[1],
                device_id_type=pl.DeviceIdType.MESH,
            )
        lax.fori_loop(
            0, 2 * (ring - 1), lambda j, x: (greet(distance(j // 2), lax.rem(j, 2)), x)[1], 0
        )
    greet(0, 1)

    table = jnp.zeros((toks, experts), F32)
    lane = iota((toks, experts), 1)
    for k in range(ids_ref.shape[1]):
        table = table + jnp.where(
            ids_ref[:, k:k + 1] == lane, gates_ref[:, k:k + 1].astype(F32), 0.0
        )
    table = table.astype(BF16)
    g_own[...] = table
    for path in range(2):
        g_in[path, near_me(path)] = table
    for s in range(STREAMS):
        in1[s, near_me(path_of(s))] = tok_ref[:, s * cols:(s + 1) * cols]

    pl.semaphore_wait(barrier, 4 * (ring - 1) + 1)

    for path in range(2):
        def send_table(d, path=path):
            remote(
                g_own, g_in.at[path, near_me(path)], g_send.at[path], g_recv.at[path],
                near(path, d)[1],
            ).start()
        each_near(send_table)
    for s in range(STREAMS):
        def send_rows(d, s=s, path=path_of(s)):
            remote(
                tok_ref.at[:, pl.ds(s * cols, cols)], in1.at[s, near_me(path)],
                send1.at[s], recv1.at[s], near(path, d)[1],
            ).start()
        each_near(send_rows)

    for path in range(2):
        wait_bytes(g_in.at[path], ring - 1, g_recv.at[path])
        gates = g_in[path].reshape(rows1, experts)
        named = jnp.where(gates.astype(F32) > 0, 1.0, 0.0).astype(BF16)
        r, q = iota((rows1, rows1), 0), iota((rows1, rows1), 1)
        below = jnp.where((r // toks == q // toks) & (q < r), 1.0, 0.0).astype(BF16)
        rank = dot(below, named).astype(BF16)

        def expert_of(slot, path=path):
            block = slot // blocks
            if path == 0:
                return z * blocks + block
            return (block // 2) * blocks + y * 2 + lax.rem(block, 2)

        pick = jnp.where(
            iota((experts, rows2), 0) == expert_of(iota((experts, rows2), 1)), 1.0, 0.0
        ).astype(BF16)
        row, slot = iota((rows1, rows2), 0), iota((rows1, rows2), 1)
        fits = (row // toks == lax.rem(slot // 2, ring)) & (
            dot(rank, pick) == lax.rem(slot, 2).astype(F32)
        )
        c_tab[path] = jnp.where(fits, dot(gates, pick), 0.0).astype(BF16)
        pick_t = jnp.where(
            iota((rows2, experts), 1) == expert_of(iota((rows2, experts), 0)), 1.0, 0.0
        ).astype(BF16)
        row, slot = iota((rows2, rows1), 1), iota((rows2, rows1), 0)
        fits = (row // toks == lax.rem(slot // 2, ring)) & (
            dot_nt(pick_t, rank) == lax.rem(slot, 2).astype(F32)
        )
        s_tab[path] = jnp.where(fits & (dot_nt(pick_t, gates) > 0), 1.0, 0.0).astype(BF16)

    for s in range(STREAMS):
        path = path_of(s)
        wait_bytes(in1.at[s], ring - 1, recv1.at[s])
        chosen = dot(s_tab[path], in1[s].reshape(rows1, cols)).astype(BF16)
        out2[s] = chosen.reshape(blocks, blocks, cols)
        in2[s, far_me(path)] = out2[s, far_me(path)]

        def send_chosen(d, f, s=s, path=path):
            to, device = far(path, d, f)
            remote(
                out2.at[s, to], in2.at[s, far_me(path)], send2.at[s], recv2.at[s], device
            ).start()
        each_far(send_chosen)

    r, q = iota((rows2, rows2), 0), iota((rows2, rows2), 1)
    swapped = (
        lax.rem(r // 2, ring) * (2 * blocks)
        + lax.rem(r // blocks, 2) * blocks
        + (r // (2 * blocks)) * 2
        + lax.rem(r, 2)
    )
    swap = jnp.where(q == swapped, 1.0, 0.0).astype(BF16)

    for s in range(STREAMS):
        wait_bytes(in2.at[s], blocks - 1, recv2.at[s])
        rows = in2[s].reshape(rows2, cols)
        if path_of(s) == 1:
            rows = dot(swap, rows).astype(BF16)
        if s == 0:
            loads[0].wait()
            loads[1].wait()

        def project(j, x, s=s, rows=rows):
            at = pl.ds(pl.multiple_of(j * TILE, TILE), TILE)
            gate_part = dot(rows, wg[s * cols:(s + 1) * cols, at])
            up_part = dot(rows, wu[s * cols:(s + 1) * cols, at])
            if s > 0:
                gate_part = gate_part + acc_g[:, at]
                up_part = up_part + acc_u[:, at]
            if s < STREAMS - 1:
                acc_g[:, at] = gate_part
                acc_u[:, at] = up_part
            else:
                hid[0, :, at] = (gate_part * jax.nn.sigmoid(gate_part) * up_part).astype(BF16)
            return x
        lax.fori_loop(0, ff // TILE, project, 0)
    hid[1] = dot(swap, hid[0]).astype(BF16)
    loads[2].wait()

    for s in range(STREAMS):
        path = path_of(s)
        hidden = hid[path]

        def down(j, x, s=s, hidden=hidden):
            at = pl.ds(pl.multiple_of(j * TILE, TILE), TILE)
            here = pl.ds(pl.multiple_of(s * cols + j * TILE, TILE), TILE)
            out3[s, :, :, at] = dot(hidden, wd[:, here]).astype(BF16).reshape(
                blocks, blocks, TILE
            )
            return x
        lax.fori_loop(0, cols // TILE, down, 0)
        in3[s, far_me(path)] = out3[s, far_me(path)]

        def send_back(d, f, s=s, path=path):
            to, device = far(path, d, f)
            remote(
                out3.at[s, to], in3.at[s, far_me(path)], send3.at[s], recv3.at[s], device
            ).start()
        each_far(send_back)

    for s in range(STREAMS):
        path = path_of(s)
        wait_bytes(in3.at[s], blocks - 1, recv3.at[s])
        summed = dot(c_tab[path], in3[s].reshape(rows2, cols)).astype(BF16)
        out4[s] = summed.reshape(ring, toks, cols)
        in4[s, near_me(path)] = out4[s, near_me(path)]

        def send_sum(d, s=s, path=path):
            to, device = near(path, d)
            remote(
                out4.at[s, to], in4.at[s, near_me(path)], send4.at[s], recv4.at[s], device
            ).start()
        each_near(send_sum)

    for s in range(STREAMS):
        wait_bytes(in4.at[s], ring - 1, recv4.at[s])
        total = in4[s, 0].astype(F32)
        for i in range(1, ring):
            total = total + in4[s, i].astype(F32)
        o_ref[:, s * cols:(s + 1) * cols] = total

    for path in range(2):
        wait_bytes(g_in.at[path], ring - 1, g_send.at[path])
    for s in range(STREAMS):
        wait_bytes(in1.at[s], ring - 1, send1.at[s])
        wait_bytes(out2.at[s], blocks - 1, send2.at[s])
        wait_bytes(out3.at[s], blocks - 1, send3.at[s])
        wait_bytes(out4.at[s], ring - 1, send4.at[s])


def shards(tokens, expert_ids, gate_weights, w_gate, w_up, w_down):
    toks, width = tokens.shape
    ff = w_gate.shape[2]
    ring = lax.axis_size("grp")
    blocks = lax.axis_size("exp")
    assert blocks == 2 * ring
    experts = ring * blocks
    rows1, rows2 = ring * toks, blocks * blocks
    cols = width // STREAMS
    vmem = pl.BlockSpec(memory_space=pltpu.VMEM)
    hbm = pl.BlockSpec(memory_space=pl.ANY)
    wide = pltpu.VMEM((STREAMS, blocks, blocks, cols), BF16)
    narrow = pltpu.VMEM((STREAMS, ring, toks, cols), BF16)
    sems = pltpu.SemaphoreType.DMA((STREAMS,))
    return pl.pallas_call(
        functools.partial(kernel, ring),
        out_shape=jax.ShapeDtypeStruct((toks, width), F32),
        in_specs=[vmem, vmem, vmem, hbm, hbm, hbm],
        out_specs=vmem,
        scratch_shapes=[
            pltpu.VMEM((toks, experts), BF16),
            pltpu.VMEM((2, ring, toks, experts), BF16),
            pltpu.VMEM((2, rows1, rows2), BF16),
            pltpu.VMEM((2, rows2, rows1), BF16),
            narrow, wide, wide, wide, wide, narrow, narrow,
            pltpu.VMEM((width, ff), BF16),
            pltpu.VMEM((width, ff), BF16),
            pltpu.VMEM((ff, width), BF16),
            pltpu.VMEM((rows2, ff), F32),
            pltpu.VMEM((rows2, ff), F32),
            pltpu.VMEM((2, rows2, ff), BF16),
            pltpu.SemaphoreType.DMA((3,)),
            pltpu.SemaphoreType.DMA((2,)),
            pltpu.SemaphoreType.DMA((2,)),
            sems, sems, sems, sems, sems, sems, sems, sems,
        ],
        compiler_params=pltpu.CompilerParams(
            collective_id=0, has_side_effects=True, vmem_limit_bytes=48 * 1024 * 1024
        ),
    )(expert_ids, gate_weights, tokens, w_gate[0], w_up[0], w_down[0])


def solution(mesh):
    return jax.shard_map(
        shards,
        mesh=mesh,
        in_specs=(
            P(("rep", "grp", "exp"), None),
            P(("rep", "grp", "exp"), None),
            P(("rep", "grp", "exp"), None),
            P(("grp", "exp"), None, None),
            P(("grp", "exp"), None, None),
            P(("grp", "exp"), None, None),
        ),
        out_specs=P(("rep", "grp", "exp"), None),
        check_vma=False,
    )
```

```python
import functools
import jax
import jax.numpy as jnp
from jax import lax
from jax.experimental import pallas as pl
from jax.experimental.pallas import tpu as pltpu
from jax.sharding import PartitionSpec as P

F32 = jnp.float32
BF16 = jnp.bfloat16
STREAMS = 4
SLOTS = 2
TILE = 256
VMEM_BYTES = 67043328


def iota(shape, dim):
    return lax.broadcasted_iota(jnp.int32, shape, dim)


def dot(a, b):
    return jnp.dot(a, b, preferred_element_type=F32)


def dot_nt(a, b):
    return lax.dot_general(a, b, (((1,), (1,)), ((), ())), preferred_element_type=F32)


def kernel(
    ring,
    ids_hbm, gates_hbm, tok_hbm, wg_hbm, wu_hbm, wd_hbm, o_ref,
    ids_ref, gates_ref, tok_ref, g_own, g_in, c_tab, s_tab, in1, out2, in2, out3, in3, out4, in4,
    wg, wu, wd, acc_g, acc_u, hid,
    x_sem, w_sem, g_send, g_recv, send1, recv1, send2, recv2, send3, recv3, send4, recv4,
):
    toks, width = tok_hbm.shape
    ff = wg.shape[1]
    blocks = 2 * ring
    rows2 = blocks * ring
    rows1 = ring * toks
    experts = ring * blocks
    cols = width // STREAMS
    z = lax.axis_index("grp")
    e = lax.axis_index("exp")
    y = lax.div(e, 2)
    c = lax.rem(e, 2)

    def path_of(s):
        return s % 2

    order = [ring // 2 + ((j + 1) // 2) * (1 - 2 * (j % 2)) for j in range(ring - 1)]
    zs = {d: lax.rem(z + d, ring) for d in order}
    ys = {d: lax.rem(y + d, ring) * 2 for d in order}
    flip = 1 - c
    near_me = (z, y)
    far_me = (e, z * 2 + c)
    near = (
        [(zs[d], {"grp": zs[d], "exp": e}) for d in order],
        [(lax.div(ys[d], 2), {"grp": z, "exp": ys[d] + c}) for d in order],
    )
    far = (
        [(ys[d] + k, {"grp": z, "exp": ys[d] + k}) for d in order for k in (c, flip)]
        + [(y * 2 + flip, {"grp": z, "exp": y * 2 + flip})],
        [(zs[d] * 2 + k, {"grp": zs[d], "exp": y * 2 + k}) for d in order for k in (c, flip)]
        + [(z * 2 + flip, {"grp": z, "exp": y * 2 + flip})],
    )

    def remote(src, dst, send, recv, device):
        return pltpu.make_async_remote_copy(
            src_ref=src, dst_ref=dst, send_sem=send, recv_sem=recv,
            device_id=device, device_id_type=pl.DeviceIdType.MESH,
        )

    def wait_bytes(ref, count, sem):
        part = ref.at[pl.ds(0, count)]
        pltpu.make_async_copy(part, part, sem).wait()

    inputs = [
        pltpu.make_async_copy(hbm, vmem, x_sem.at[i])
        for i, (hbm, vmem) in enumerate(
            ((ids_hbm, ids_ref), (gates_hbm, gates_ref), (tok_hbm, tok_ref))
        )
    ]
    for copy in inputs:
        copy.start()

    barrier = pltpu.get_barrier_semaphore()

    for _, device in far[0] + far[1][:-1]:
        pl.semaphore_signal(
            barrier, inc=1, device_id=device, device_id_type=pl.DeviceIdType.MESH
        )

    inputs[0].wait()
    inputs[1].wait()
    table = jnp.zeros((experts, toks), F32)
    expert = iota((experts, toks), 0)
    for k in range(ids_ref.shape[0]):
        table = table + jnp.where(
            ids_ref[k:k + 1, :] == expert, gates_ref[k:k + 1, :].astype(F32), 0.0
        )
    same = jnp.where(iota((toks, toks), 0) == iota((toks, toks), 1), 1.0, 0.0).astype(BF16)
    table = dot_nt(same, table.astype(BF16)).astype(BF16)
    g_own[...] = table
    for path in range(2):
        g_in[path, near_me[path]] = table
    inputs[2].wait()

    pl.semaphore_wait(barrier, 4 * (ring - 1) + 1)

    for path in range(2):
        for _, device in near[path]:
            remote(
                g_own, g_in.at[path, near_me[path]], g_send.at[path], g_recv.at[path], device
            ).start()
    for s in range(STREAMS):
        path = path_of(s)
        for _, device in near[path]:
            remote(
                tok_ref.at[:, pl.ds(s * cols, cols)], in1.at[s, near_me[path]],
                send1.at[s], recv1.at[s], device,
            ).start()

    loads = [
        pltpu.make_async_copy(hbm, vmem, w_sem.at[i])
        for i, (hbm, vmem) in enumerate(((wg_hbm, wg), (wu_hbm, wu), (wd_hbm, wd)))
    ]
    for load in loads:
        load.start()
    for s in range(STREAMS):
        in1[s, near_me[path_of(s)]] = tok_ref[:, s * cols:(s + 1) * cols]

    for path in range(2):
        wait_bytes(g_in.at[path], ring - 1, g_recv.at[path])
        gates = g_in[path].reshape(rows1, experts)
        named = jnp.where(gates.astype(F32) > 0, 1.0, 0.0).astype(BF16)
        r, q = iota((rows1, rows1), 0), iota((rows1, rows1), 1)
        below = jnp.where((r // toks == q // toks) & (q < r), 1.0, 0.0).astype(BF16)
        rank = dot(below, named).astype(BF16)

        def expert_of(place, path=path):
            block = place // ring
            if path == 0:
                return z * blocks + block
            return (block // 2) * blocks + y * 2 + lax.rem(block, 2)

        pick = jnp.where(
            iota((experts, rows2), 0) == expert_of(iota((experts, rows2), 1)), 1.0, 0.0
        ).astype(BF16)
        own = iota((rows1, rows2), 0) // toks == lax.rem(iota((rows1, rows2), 1), ring)
        value, place = dot(gates, pick), dot(rank, pick)
        for b in range(SLOTS):
            c_tab[path, b] = jnp.where(own & (place == b), value, 0.0).astype(BF16)
        pick = jnp.where(
            iota((rows2, experts), 1) == expert_of(iota((rows2, experts), 0)), 1.0, 0.0
        ).astype(BF16)
        own = iota((rows2, rows1), 1) // toks == lax.rem(iota((rows2, rows1), 0), ring)
        own = own & (dot_nt(pick, gates) > 0)
        place = dot_nt(pick, rank)
        for b in range(SLOTS):
            s_tab[path, b] = jnp.where(own & (place == b), 1.0, 0.0).astype(BF16)

    for b in range(SLOTS):
        for s in range(STREAMS):
            path, n = path_of(s), b * STREAMS + s
            if b == 0:
                wait_bytes(in1.at[s], ring - 1, recv1.at[s])
            chosen = dot(s_tab[path, b], in1[s].reshape(rows1, cols)).astype(BF16)
            out2[n] = chosen.reshape(blocks, ring, cols)
            in2[n, far_me[path]] = out2[n, far_me[path]]

            for to, device in far[path]:
                remote(
                    out2.at[n, to], in2.at[n, far_me[path]], send2.at[n], recv2.at[n], device
                ).start()

    r, q = iota((rows2, rows2), 0), iota((rows2, rows2), 1)
    swapped = (
        lax.rem(r, ring) * blocks + lax.rem(r // ring, 2) * ring + r // blocks
    )
    swap = jnp.where(q == swapped, 1.0, 0.0).astype(BF16)

    for b in range(SLOTS):
        for s in range(STREAMS):
            n = b * STREAMS + s
            wait_bytes(in2.at[n], blocks - 1, recv2.at[n])
            rows = in2[n].reshape(rows2, cols)
            if path_of(s) == 1:
                rows = dot(swap, rows).astype(BF16)
            if n == 0:
                loads[0].wait()
                loads[1].wait()

            def project(j, x, s=s, rows=rows):
                at = pl.ds(pl.multiple_of(j * TILE, TILE), TILE)
                gate_part = dot(rows, wg[s * cols:(s + 1) * cols, at])
                up_part = dot(rows, wu[s * cols:(s + 1) * cols, at])
                if s > 0:
                    gate_part = gate_part + acc_g[:, at]
                    up_part = up_part + acc_u[:, at]
                if s < STREAMS - 1:
                    acc_g[:, at] = gate_part
                    acc_u[:, at] = up_part
                else:
                    hid[0, :, at] = (
                        gate_part * jax.nn.sigmoid(gate_part) * up_part
                    ).astype(BF16)
                return x
            lax.fori_loop(0, ff // TILE, project, 0)
        hid[1] = dot(swap, hid[0]).astype(BF16)
        if b == 0:
            loads[2].wait()

        for s in range(STREAMS):
            path, n = path_of(s), b * STREAMS + s
            hidden = hid[path]

            def down(j, x, s=s, n=n, hidden=hidden):
                at = pl.ds(pl.multiple_of(j * TILE, TILE), TILE)
                here = pl.ds(pl.multiple_of(s * cols + j * TILE, TILE), TILE)
                out3[n, :, :, at] = dot(hidden, wd[:, here]).astype(BF16).reshape(
                    blocks, ring, TILE
                )
                return x
            lax.fori_loop(0, cols // TILE, down, 0)
            in3[n, far_me[path]] = out3[n, far_me[path]]

            for to, device in far[path]:
                remote(
                    out3.at[n, to], in3.at[n, far_me[path]], send3.at[n], recv3.at[n], device
                ).start()

    for s in range(STREAMS):
        path = path_of(s)
        summed = jnp.zeros((rows1, cols), F32)
        for b in range(SLOTS):
            n = b * STREAMS + s
            wait_bytes(in3.at[n], blocks - 1, recv3.at[n])
            summed = summed + dot(c_tab[path, b], in3[n].reshape(rows2, cols))
        out4[s] = summed.astype(BF16).reshape(ring, toks, cols)
        in4[s, near_me[path]] = out4[s, near_me[path]]

        for to, device in near[path]:
            remote(
                out4.at[s, to], in4.at[s, near_me[path]], send4.at[s], recv4.at[s], device
            ).start()

    for s in range(STREAMS):
        wait_bytes(in4.at[s], ring - 1, recv4.at[s])
        total = in4[s, 0].astype(F32)
        for i in range(1, ring):
            total = total + in4[s, i].astype(F32)
        o_ref[:, s * cols:(s + 1) * cols] = total

    for path in range(2):
        wait_bytes(g_in.at[path], ring - 1, g_send.at[path])
    for s in range(STREAMS):
        wait_bytes(in1.at[s], ring - 1, send1.at[s])
        wait_bytes(out4.at[s], ring - 1, send4.at[s])
    for n in range(SLOTS * STREAMS):
        wait_bytes(out2.at[n], blocks - 1, send2.at[n])
        wait_bytes(out3.at[n], blocks - 1, send3.at[n])


def shards(tokens, expert_ids, gate_weights, w_gate, w_up, w_down):
    toks, width = tokens.shape
    ff = w_gate.shape[2]
    ring = lax.axis_size("grp")
    blocks = lax.axis_size("exp")
    assert blocks == 2 * ring
    experts = ring * blocks
    rows1, rows2 = ring * toks, blocks * ring
    cols = width // STREAMS
    vmem = pl.BlockSpec(memory_space=pltpu.VMEM)
    hbm = pl.BlockSpec(memory_space=pl.ANY)
    wide = pltpu.VMEM((SLOTS * STREAMS, blocks, ring, cols), BF16)
    narrow = pltpu.VMEM((STREAMS, ring, toks, cols), BF16)
    sems = pltpu.SemaphoreType.DMA((STREAMS,))
    more = pltpu.SemaphoreType.DMA((SLOTS * STREAMS,))
    return pl.pallas_call(
        functools.partial(kernel, ring),
        out_shape=jax.ShapeDtypeStruct((toks, width), F32),
        in_specs=[hbm] * 6,
        out_specs=vmem,
        scratch_shapes=[
            pltpu.VMEM(expert_ids.shape[::-1], jnp.int32),
            pltpu.VMEM(expert_ids.shape[::-1], BF16),
            pltpu.VMEM((toks, width), BF16),
            pltpu.VMEM((toks, experts), BF16),
            pltpu.VMEM((2, ring, toks, experts), BF16),
            pltpu.VMEM((2, SLOTS, rows1, rows2), BF16),
            pltpu.VMEM((2, SLOTS, rows2, rows1), BF16),
            narrow, wide, wide, wide, wide, narrow, narrow,
            pltpu.VMEM((width, ff), BF16),
            pltpu.VMEM((width, ff), BF16),
            pltpu.VMEM((ff, width), BF16),
            pltpu.VMEM((rows2, ff), F32),
            pltpu.VMEM((rows2, ff), F32),
            pltpu.VMEM((2, rows2, ff), BF16),
            pltpu.SemaphoreType.DMA((3,)),
            pltpu.SemaphoreType.DMA((3,)),
            pltpu.SemaphoreType.DMA((2,)),
            pltpu.SemaphoreType.DMA((2,)),
            sems, sems, more, more, more, more, sems, sems,
        ],
        compiler_params=pltpu.CompilerParams(
            collective_id=0, has_side_effects=True, vmem_limit_bytes=VMEM_BYTES
        ),
    )(expert_ids.T, gate_weights.T, tokens, w_gate[0], w_up[0], w_down[0])


def solution(mesh):
    return jax.shard_map(
        shards,
        mesh=mesh,
        in_specs=(
            P(("rep", "grp", "exp"), None),
            P(("rep", "grp", "exp"), None),
            P(("rep", "grp", "exp"), None),
            P(("grp", "exp"), None, None),
            P(("grp", "exp"), None, None),
            P(("grp", "exp"), None, None),
        ),
        out_specs=P(("rep", "grp", "exp"), None),
        check_vma=False,
    )
```

```python
import functools
import jax
import jax.numpy as jnp
from jax import lax
from jax.experimental import pallas as pl
from jax.experimental.pallas import tpu as pltpu
from jax.sharding import PartitionSpec as P

F32 = jnp.float32
BF16 = jnp.bfloat16
CUTS = (512,)
BACK = 1
SLOTS = 2
TILE = 256
VMEM_BYTES = 48 * 1024 * 1024


def iota(shape, dim):
    return lax.broadcasted_iota(jnp.int32, shape, dim)


def dot(a, b):
    return jnp.dot(a, b, preferred_element_type=F32)


def dot_nt(a, b):
    return lax.dot_general(a, b, (((1,), (1,)), ((), ())), preferred_element_type=F32)


def kernel(
    ring,
    ids_hbm, gates_hbm, tok_hbm, wg_hbm, wu_hbm, wd_hbm, o_ref,
    ids_ref, gates_ref, tok_ref, g_own, g_in, c_tab, s_tab, in1, out2, in2, out3, in3, out4, in4,
    wg, wu, wd, acc_g, acc_u, hid,
    x_sem, w_sem, g_send, g_recv, send1, recv1, send2, recv2, send3, recv3, send4, recv4,
):
    toks, width = tok_hbm.shape
    ff = wg.shape[1]
    blocks = 2 * ring
    rows2 = blocks * ring
    rows1 = ring * toks
    experts = ring * blocks
    z = lax.axis_index("grp")
    e = lax.axis_index("exp")
    y = lax.div(e, 2)
    c = lax.rem(e, 2)

    half = width // 2
    edges = (0,) + CUTS + (half,)
    out_chunks = [
        (path, left, right - left) for left, right in zip(edges, edges[1:]) for path in range(2)
    ]
    back_chunks = [
        (path, left, size)
        for _, left, size in out_chunks[::2][::BACK] for path in range(2)
    ]
    chunks = len(out_chunks)

    order = [ring // 2 + ((j + 1) // 2) * (1 - 2 * (j % 2)) for j in range(ring - 1)]
    zs = {d: lax.rem(z + d, ring) for d in order}
    ys = {d: lax.rem(y + d, ring) * 2 for d in order}
    flip = 1 - c
    near_me = (z, y)
    far_me = (e, z * 2 + c)
    near = (
        [(zs[d], {"grp": zs[d], "exp": e}) for d in order],
        [(lax.div(ys[d], 2), {"grp": z, "exp": ys[d] + c}) for d in order],
    )
    far = (
        [(ys[d] + k, {"grp": z, "exp": ys[d] + k}) for d in order for k in (c, flip)]
        + [(y * 2 + flip, {"grp": z, "exp": y * 2 + flip})],
        [(zs[d] * 2 + k, {"grp": zs[d], "exp": y * 2 + k}) for d in order for k in (c, flip)]
        + [(z * 2 + flip, {"grp": z, "exp": y * 2 + flip})],
    )

    def remote(src, dst, send, recv, device):
        return pltpu.make_async_remote_copy(
            src_ref=src, dst_ref=dst, send_sem=send, recv_sem=recv,
            device_id=device, device_id_type=pl.DeviceIdType.MESH,
        )

    def wait_bytes(ref, count, sem):
        part = ref.at[pl.ds(0, count)]
        pltpu.make_async_copy(part, part, sem).wait()

    inputs = [
        pltpu.make_async_copy(hbm, vmem, x_sem.at[i])
        for i, (hbm, vmem) in enumerate(
            ((ids_hbm, ids_ref), (gates_hbm, gates_ref), (tok_hbm, tok_ref))
        )
    ]
    for copy in inputs:
        copy.start()

    barrier = pltpu.get_barrier_semaphore()

    for _, device in far[0] + far[1][:-1]:
        pl.semaphore_signal(
            barrier, inc=1, device_id=device, device_id_type=pl.DeviceIdType.MESH
        )

    inputs[0].wait()
    inputs[1].wait()
    table = jnp.zeros((experts, toks), F32)
    expert = iota((experts, toks), 0)
    for k in range(ids_ref.shape[0]):
        table = table + jnp.where(
            ids_ref[k:k + 1, :] == expert, gates_ref[k:k + 1, :].astype(F32), 0.0
        )
    same = jnp.where(iota((toks, toks), 0) == iota((toks, toks), 1), 1.0, 0.0).astype(BF16)
    table = dot_nt(same, table.astype(BF16)).astype(BF16)
    g_own[...] = table
    for path in range(2):
        g_in[path, near_me[path]] = table
    inputs[2].wait()

    pl.semaphore_wait(barrier, 4 * (ring - 1) + 1)

    for path in range(2):
        for _, device in near[path]:
            remote(
                g_own, g_in.at[path, near_me[path]], g_send.at[path], g_recv.at[path], device
            ).start()
    def block(path, source, start, size):
        return in1.at[path, source, :, pl.ds(start, size)]

    for n, (path, start, size) in enumerate(out_chunks):
        for _, device in near[path]:
            remote(
                tok_ref.at[:, pl.ds(path * half + start, size)],
                block(path, near_me[path], start, size),
                send1.at[n], recv1.at[n], device,
            ).start()

    loads = [
        pltpu.make_async_copy(hbm, vmem, w_sem.at[i])
        for i, (hbm, vmem) in enumerate(((wg_hbm, wg), (wu_hbm, wu), (wd_hbm, wd)))
    ]
    for load in loads:
        load.start()
    for path in range(2):
        in1[path, near_me[path]] = tok_ref[:, path * half:(path + 1) * half]

    for path in range(2):
        wait_bytes(g_in.at[path], ring - 1, g_recv.at[path])
        gates = g_in[path].reshape(rows1, experts)
        named = jnp.where(gates.astype(F32) > 0, 1.0, 0.0).astype(BF16)
        r, q = iota((rows1, rows1), 0), iota((rows1, rows1), 1)
        below = jnp.where((r // toks == q // toks) & (q < r), 1.0, 0.0).astype(BF16)
        rank = dot(below, named).astype(BF16)

        def expert_of(place, path=path):
            block = place // ring
            if path == 0:
                return z * blocks + block
            return (block // 2) * blocks + y * 2 + lax.rem(block, 2)

        pick = jnp.where(
            iota((experts, rows2), 0) == expert_of(iota((experts, rows2), 1)), 1.0, 0.0
        ).astype(BF16)
        own = iota((rows1, rows2), 0) // toks == lax.rem(iota((rows1, rows2), 1), ring)
        value, place = dot(gates, pick), dot(rank, pick)
        for b in range(SLOTS):
            c_tab[path, b] = jnp.where(own & (place == b), value, 0.0).astype(BF16)
        pick = jnp.where(
            iota((rows2, experts), 1) == expert_of(iota((rows2, experts), 0)), 1.0, 0.0
        ).astype(BF16)
        own = iota((rows2, rows1), 1) // toks == lax.rem(iota((rows2, rows1), 0), ring)
        own = own & (dot_nt(pick, gates) > 0)
        place = dot_nt(pick, rank)
        for b in range(SLOTS):
            s_tab[path, b] = jnp.where(own & (place == b), 1.0, 0.0).astype(BF16)

    for b in range(SLOTS):
        for i, (path, start, size) in enumerate(out_chunks):
            n = b * chunks + i
            at = slice(start, start + size)
            if b == 0:
                wait_bytes(in1.at[path, :, :, pl.ds(start, size)], ring - 1, recv1.at[i])
            rows = in1[path, :, :, at].reshape(rows1, size)
            chosen = dot(s_tab[path, b], rows).astype(BF16)
            out2[b, path, :, :, at] = chosen.reshape(blocks, ring, size)
            in2[b, path, far_me[path], :, at] = out2[b, path, far_me[path], :, at]
            for to, device in far[path]:
                remote(
                    out2.at[b, path, to, :, pl.ds(start, size)],
                    in2.at[b, path, far_me[path], :, pl.ds(start, size)],
                    send2.at[n], recv2.at[n], device,
                ).start()

    r, q = iota((rows2, rows2), 0), iota((rows2, rows2), 1)
    swapped = (
        lax.rem(r, ring) * blocks + lax.rem(r // ring, 2) * ring + r // blocks
    )
    swap = jnp.where(q == swapped, 1.0, 0.0).astype(BF16)

    for b in range(SLOTS):
        last = len(out_chunks) - 1
        for i, (path, start, size) in enumerate(out_chunks):
            n = b * chunks + i
            wait_bytes(in2.at[b, path, :, :, pl.ds(start, size)], blocks - 1, recv2.at[n])
            rows = in2[b, path, :, :, start:start + size].reshape(rows2, size)
            if path == 1:
                rows = dot(swap, rows).astype(BF16)
            if n == 0:
                loads[0].wait()
                loads[1].wait()

            def project(j, x, i=i, rows=rows, top=path * half + start, size=size, last=last):
                at = pl.ds(pl.multiple_of(j * TILE, TILE), TILE)
                gate_part = dot(rows, wg[top:top + size, at])
                up_part = dot(rows, wu[top:top + size, at])
                if i > 0:
                    gate_part = gate_part + acc_g[:, at]
                    up_part = up_part + acc_u[:, at]
                if i < last:
                    acc_g[:, at] = gate_part
                    acc_u[:, at] = up_part
                else:
                    hid[0, :, at] = (
                        gate_part * jax.nn.sigmoid(gate_part) * up_part
                    ).astype(BF16)
                return x
            lax.fori_loop(0, ff // TILE, project, 0)
        hid[1] = dot(swap, hid[0]).astype(BF16)
        if b == 0:
            loads[2].wait()

        for i, (path, start, size) in enumerate(back_chunks):
            n = b * chunks + i
            hidden = hid[path]

            def down(j, x, b=b, path=path, start=start, hidden=hidden):
                at = pl.ds(pl.multiple_of(start + j * TILE, TILE), TILE)
                here = pl.ds(pl.multiple_of(path * half + start + j * TILE, TILE), TILE)
                out3[b, path, :, :, at] = dot(hidden, wd[:, here]).astype(BF16).reshape(
                    blocks, ring, TILE
                )
                return x
            lax.fori_loop(0, size // TILE, down, 0)
            at = slice(start, start + size)
            in3[b, path, far_me[path], :, at] = out3[b, path, far_me[path], :, at]
            for to, device in far[path]:
                remote(
                    out3.at[b, path, to, :, pl.ds(start, size)],
                    in3.at[b, path, far_me[path], :, pl.ds(start, size)],
                    send3.at[n], recv3.at[n], device,
                ).start()

    for n, (path, start, size) in enumerate(back_chunks):
        summed = jnp.zeros((rows1, size), F32)
        at = slice(start, start + size)
        for b in range(SLOTS):
            wait_bytes(
                in3.at[b, path, :, :, pl.ds(start, size)], blocks - 1, recv3.at[b * chunks + n]
            )
            back = in3[b, path, :, :, at].reshape(rows2, size)
            summed = summed + dot(c_tab[path, b], back)
        out4[path, :, :, at] = summed.astype(BF16).reshape(ring, toks, size)
        in4[path, near_me[path], :, at] = out4[path, near_me[path], :, at]
        for to, device in near[path]:
            remote(
                out4.at[path, to, :, pl.ds(start, size)],
                in4.at[path, near_me[path], :, pl.ds(start, size)],
                send4.at[n], recv4.at[n], device,
            ).start()

    for n, (path, start, size) in enumerate(back_chunks):
        wait_bytes(in4.at[path, :, :, pl.ds(start, size)], ring - 1, recv4.at[n])
        at = slice(start, start + size)
        total = in4[path, 0, :, at].astype(F32)
        for i in range(1, ring):
            total = total + in4[path, i, :, at].astype(F32)
        o_ref[:, path * half + start:path * half + start + size] = total

    for path in range(2):
        wait_bytes(g_in.at[path], ring - 1, g_send.at[path])
    for n, (path, start, size) in enumerate(out_chunks):
        wait_bytes(in1.at[path, :, :, pl.ds(start, size)], ring - 1, send1.at[n])
        for b in range(SLOTS):
            part = out2.at[b, path, :, :, pl.ds(start, size)]
            wait_bytes(part, blocks - 1, send2.at[b * chunks + n])
    for n, (path, start, size) in enumerate(back_chunks):
        wait_bytes(out4.at[path, :, :, pl.ds(start, size)], ring - 1, send4.at[n])
        for b in range(SLOTS):
            part = out3.at[b, path, :, :, pl.ds(start, size)]
            wait_bytes(part, blocks - 1, send3.at[b * chunks + n])


def shards(tokens, expert_ids, gate_weights, w_gate, w_up, w_down):
    toks, width = tokens.shape
    ff = w_gate.shape[2]
    ring = lax.axis_size("grp")
    blocks = lax.axis_size("exp")
    assert blocks == 2 * ring
    experts = ring * blocks
    rows1, rows2 = ring * toks, blocks * ring
    vmem = pl.BlockSpec(memory_space=pltpu.VMEM)
    hbm = pl.BlockSpec(memory_space=pl.ANY)
    wide = pltpu.VMEM((SLOTS, 2, blocks, ring, width // 2), BF16)
    narrow = pltpu.VMEM((2, ring, toks, width // 2), BF16)
    sems = pltpu.SemaphoreType.DMA((2 * len(CUTS) + 2,))
    more = pltpu.SemaphoreType.DMA((SLOTS * (2 * len(CUTS) + 2),))
    return pl.pallas_call(
        functools.partial(kernel, ring),
        out_shape=jax.ShapeDtypeStruct((toks, width), F32),
        in_specs=[hbm] * 6,
        out_specs=vmem,
        scratch_shapes=[
            pltpu.VMEM(expert_ids.shape[::-1], jnp.int32),
            pltpu.VMEM(expert_ids.shape[::-1], BF16),
            pltpu.VMEM((toks, width), BF16),
            pltpu.VMEM((toks, experts), BF16),
            pltpu.VMEM((2, ring, toks, experts), BF16),
            pltpu.VMEM((2, SLOTS, rows1, rows2), BF16),
            pltpu.VMEM((2, SLOTS, rows2, rows1), BF16),
            narrow, wide, wide, wide, wide, narrow, narrow,
            pltpu.VMEM((width, ff), BF16),
            pltpu.VMEM((width, ff), BF16),
            pltpu.VMEM((ff, width), BF16),
            pltpu.VMEM((rows2, ff), F32),
            pltpu.VMEM((rows2, ff), F32),
            pltpu.VMEM((2, rows2, ff), BF16),
            pltpu.SemaphoreType.DMA((3,)),
            pltpu.SemaphoreType.DMA((3,)),
            pltpu.SemaphoreType.DMA((2,)),
            pltpu.SemaphoreType.DMA((2,)),
            sems, sems, more, more, more, more, sems, sems,
        ],
        compiler_params=pltpu.CompilerParams(
            collective_id=0, has_side_effects=True, vmem_limit_bytes=VMEM_BYTES
        ),
    )(*(
        pltpu.with_memory_space_constraint(x, pltpu.HBM)
        for x in (expert_ids.T, gate_weights.T, tokens, w_gate[0], w_up[0], w_down[0])
    ))


def solution(mesh):
    return jax.shard_map(
        shards,
        mesh=mesh,
        in_specs=(
            P(("rep", "grp", "exp"), None),
            P(("rep", "grp", "exp"), None),
            P(("rep", "grp", "exp"), None),
            P(("grp", "exp"), None, None),
            P(("grp", "exp"), None, None),
            P(("grp", "exp"), None, None),
        ),
        out_specs=P(("rep", "grp", "exp"), None),
        check_vma=False,
    )
```

```python
import functools
import jax
import jax.numpy as jnp
from jax import lax
from jax.experimental import pallas as pl
from jax.experimental.pallas import tpu as pltpu
from jax.sharding import PartitionSpec as P

F32 = jnp.float32
BF16 = jnp.bfloat16
CUTS = (512,)
BACK = 1
SLOTS = 2
TILE = 256
VMEM_BYTES = 48 * 1024 * 1024


def iota(shape, dim):
    return lax.broadcasted_iota(jnp.int32, shape, dim)


def dot(a, b):
    return jnp.dot(a, b, preferred_element_type=F32)


def dot_nt(a, b):
    return lax.dot_general(a, b, (((1,), (1,)), ((), ())), preferred_element_type=F32)


def kernel(
    ring,
    ids_hbm, gates_hbm, tok_hbm, wg_hbm, wu_hbm, wd_hbm, o_ref,
    ids_ref, gates_ref, tok_ref, g_own, g_in, c_tab, s_tab, in1, out2, in2, out3, in3, out4, in4,
    wg, wu, wd, acc_g, acc_u, hid, sums,
    x_sem, w_sem, g_send, g_recv, send1, recv1, send2, recv2, send3, recv3, send4, recv4,
):
    toks, width = tok_hbm.shape
    ff = wg.shape[1]
    blocks = 2 * ring
    rows2 = blocks * ring
    rows1 = ring * toks
    experts = ring * blocks
    z = lax.axis_index("grp")
    e = lax.axis_index("exp")
    y = lax.div(e, 2)
    c = lax.rem(e, 2)

    half = width // 2
    edges = (0,) + CUTS + (half,)
    out_chunks = [
        (path, left, right - left) for left, right in zip(edges, edges[1:]) for path in range(2)
    ]
    back_chunks = [
        (path, left, size)
        for _, left, size in out_chunks[::2][::BACK] for path in range(2)
    ]
    chunks = len(out_chunks)

    order = [ring // 2 + ((j + 1) // 2) * (1 - 2 * (j % 2)) for j in range(ring - 1)]
    zs = {d: lax.rem(z + d, ring) for d in order}
    ys = {d: lax.rem(y + d, ring) * 2 for d in order}
    flip = 1 - c
    near_me = (z, y)
    far_me = (e, z * 2 + c)
    near = (
        [(zs[d], {"grp": zs[d], "exp": e}) for d in order],
        [(lax.div(ys[d], 2), {"grp": z, "exp": ys[d] + c}) for d in order],
    )
    far = (
        [(ys[d] + k, {"grp": z, "exp": ys[d] + k}) for d in order for k in (c, flip)]
        + [(y * 2 + flip, {"grp": z, "exp": y * 2 + flip})],
        [(zs[d] * 2 + k, {"grp": zs[d], "exp": y * 2 + k}) for d in order for k in (c, flip)]
        + [(z * 2 + flip, {"grp": z, "exp": y * 2 + flip})],
    )

    def remote(src, dst, send, recv, device):
        return pltpu.make_async_remote_copy(
            src_ref=src, dst_ref=dst, send_sem=send, recv_sem=recv,
            device_id=device, device_id_type=pl.DeviceIdType.MESH,
        )

    def wait_bytes(ref, count, sem):
        part = ref.at[pl.ds(0, count)]
        pltpu.make_async_copy(part, part, sem).wait()

    inputs = [
        pltpu.make_async_copy(hbm, vmem, x_sem.at[i])
        for i, (hbm, vmem) in enumerate(
            ((ids_hbm, ids_ref), (gates_hbm, gates_ref), (tok_hbm, tok_ref))
        )
    ]
    for copy in inputs:
        copy.start()

    barrier = pltpu.get_barrier_semaphore()

    for _, device in far[0] + far[1][:-1]:
        pl.semaphore_signal(
            barrier, inc=1, device_id=device, device_id_type=pl.DeviceIdType.MESH
        )

    inputs[0].wait()
    inputs[1].wait()
    table = jnp.zeros((experts, toks), F32)
    expert = iota((experts, toks), 0)
    for k in range(ids_ref.shape[0]):
        table = table + jnp.where(
            ids_ref[k:k + 1, :] == expert, gates_ref[k:k + 1, :].astype(F32), 0.0
        )
    same = jnp.where(iota((toks, toks), 0) == iota((toks, toks), 1), 1.0, 0.0).astype(BF16)
    table = dot_nt(same, table.astype(BF16)).astype(BF16)
    g_own[...] = table
    for path in range(2):
        g_in[path, near_me[path]] = table
    inputs[2].wait()

    pl.semaphore_wait(barrier, 4 * (ring - 1) + 1)

    for path in range(2):
        for _, device in near[path]:
            remote(
                g_own, g_in.at[path, near_me[path]], g_send.at[path], g_recv.at[path], device
            ).start()
    def block(path, source, start, size):
        return in1.at[path, source, :, pl.ds(start, size)]

    for n, (path, start, size) in enumerate(out_chunks):
        for _, device in near[path]:
            remote(
                tok_ref.at[:, pl.ds(path * half + start, size)],
                block(path, near_me[path], start, size),
                send1.at[n], recv1.at[n], device,
            ).start()

    loads = [
        pltpu.make_async_copy(hbm, vmem, w_sem.at[i])
        for i, (hbm, vmem) in enumerate(((wg_hbm, wg), (wu_hbm, wu), (wd_hbm, wd)))
    ]
    for load in loads:
        load.start()
    for path in range(2):
        in1[path, near_me[path]] = tok_ref[:, path * half:(path + 1) * half]

    for path in range(2):
        wait_bytes(g_in.at[path], ring - 1, g_recv.at[path])
        gates = g_in[path].reshape(rows1, experts)
        named = jnp.where(gates.astype(F32) > 0, 1.0, 0.0).astype(BF16)
        r, q = iota((rows1, rows1), 0), iota((rows1, rows1), 1)
        below = jnp.where((r // toks == q // toks) & (q < r), 1.0, 0.0).astype(BF16)
        rank = dot(below, named).astype(BF16)

        def expert_of(place, path=path):
            block = place // ring
            if path == 0:
                return z * blocks + block
            return (block // 2) * blocks + y * 2 + lax.rem(block, 2)

        pick = jnp.where(
            iota((experts, rows2), 0) == expert_of(iota((experts, rows2), 1)), 1.0, 0.0
        ).astype(BF16)
        own = iota((rows1, rows2), 0) // toks == lax.rem(iota((rows1, rows2), 1), ring)
        value, place = dot(gates, pick), dot(rank, pick)
        for b in range(SLOTS):
            c_tab[path, b] = jnp.where(own & (place == b), value, 0.0).astype(BF16)
        pick = jnp.where(
            iota((rows2, experts), 1) == expert_of(iota((rows2, experts), 0)), 1.0, 0.0
        ).astype(BF16)
        own = iota((rows2, rows1), 1) // toks == lax.rem(iota((rows2, rows1), 0), ring)
        own = own & (dot_nt(pick, gates) > 0)
        place = dot_nt(pick, rank)
        for b in range(SLOTS):
            s_tab[path, b] = jnp.where(own & (place == b), 1.0, 0.0).astype(BF16)

    for b in range(SLOTS):
        for i, (path, start, size) in enumerate(out_chunks):
            n = b * chunks + i
            at = slice(start, start + size)
            if b == 0:
                wait_bytes(in1.at[path, :, :, pl.ds(start, size)], ring - 1, recv1.at[i])
            rows = in1[path, :, :, at].reshape(rows1, size)
            chosen = dot(s_tab[path, b], rows).astype(BF16)
            out2[b, path, :, :, at] = chosen.reshape(blocks, ring, size)
            in2[b, path, far_me[path], :, at] = out2[b, path, far_me[path], :, at]
            for to, device in far[path]:
                remote(
                    out2.at[b, path, to, :, pl.ds(start, size)],
                    in2.at[b, path, far_me[path], :, pl.ds(start, size)],
                    send2.at[n], recv2.at[n], device,
                ).start()

    r, q = iota((rows2, rows2), 0), iota((rows2, rows2), 1)
    swapped = (
        lax.rem(r, ring) * blocks + lax.rem(r // ring, 2) * ring + r // blocks
    )
    swap = jnp.where(q == swapped, 1.0, 0.0).astype(BF16)

    for b in range(SLOTS):
        last = len(out_chunks) - 1
        for i, (path, start, size) in enumerate(out_chunks):
            n = b * chunks + i
            wait_bytes(in2.at[b, path, :, :, pl.ds(start, size)], blocks - 1, recv2.at[n])
            rows = in2[b, path, :, :, start:start + size].reshape(rows2, size)
            if path == 1:
                rows = dot(swap, rows).astype(BF16)
            if n == 0:
                loads[0].wait()
                loads[1].wait()

            def project(j, x, i=i, rows=rows, top=path * half + start, size=size, last=last):
                at = pl.ds(pl.multiple_of(j * TILE, TILE), TILE)
                gate_part = dot(rows, wg[top:top + size, at])
                up_part = dot(rows, wu[top:top + size, at])
                if i > 0:
                    gate_part = gate_part + acc_g[:, at]
                    up_part = up_part + acc_u[:, at]
                if i < last:
                    acc_g[:, at] = gate_part
                    acc_u[:, at] = up_part
                else:
                    hid[0, :, at] = (
                        gate_part * jax.nn.sigmoid(gate_part) * up_part
                    ).astype(BF16)
                return x
            lax.fori_loop(0, ff // TILE, project, 0)
        hid[1] = dot(swap, hid[0]).astype(BF16)
        if b == 0:
            loads[2].wait()

        for i, (path, start, size) in enumerate(back_chunks):
            n = b * chunks + i
            hidden = hid[path]

            def down(j, x, b=b, path=path, start=start, hidden=hidden):
                at = pl.ds(pl.multiple_of(start + j * TILE, TILE), TILE)
                here = pl.ds(pl.multiple_of(path * half + start + j * TILE, TILE), TILE)
                out3[b, path, :, :, at] = dot(hidden, wd[:, here]).astype(BF16).reshape(
                    blocks, ring, TILE
                )
                return x
            lax.fori_loop(0, size // TILE, down, 0)
            at = slice(start, start + size)
            in3[b, path, far_me[path], :, at] = out3[b, path, far_me[path], :, at]
            for to, device in far[path]:
                remote(
                    out3.at[b, path, to, :, pl.ds(start, size)],
                    in3.at[b, path, far_me[path], :, pl.ds(start, size)],
                    send3.at[n], recv3.at[n], device,
                ).start()

    def weigh(b, n, path, start, size):
        part = in3.at[b, path, :, :, pl.ds(start, size)]
        wait_bytes(part, blocks - 1, recv3.at[b * chunks + n])
        back = in3[b, path, :, :, start:start + size].reshape(rows2, size)
        return dot(c_tab[path, b], back)

    for n, (path, start, size) in enumerate(back_chunks):
        sums[path, :, start:start + size] = weigh(0, n, path, start, size)
    for n, (path, start, size) in enumerate(back_chunks):
        at = slice(start, start + size)
        summed = sums[path, :, at] + weigh(1, n, path, start, size)
        out4[path, :, :, at] = summed.astype(BF16).reshape(ring, toks, size)
        in4[path, near_me[path], :, at] = out4[path, near_me[path], :, at]
        for to, device in near[path]:
            remote(
                out4.at[path, to, :, pl.ds(start, size)],
                in4.at[path, near_me[path], :, pl.ds(start, size)],
                send4.at[n], recv4.at[n], device,
            ).start()

    for n, (path, start, size) in enumerate(back_chunks):
        wait_bytes(in4.at[path, :, :, pl.ds(start, size)], ring - 1, recv4.at[n])
        at = slice(start, start + size)
        total = in4[path, 0, :, at].astype(F32)
        for i in range(1, ring):
            total = total + in4[path, i, :, at].astype(F32)
        o_ref[:, path * half + start:path * half + start + size] = total

    for path in range(2):
        wait_bytes(g_in.at[path], ring - 1, g_send.at[path])
    for n, (path, start, size) in enumerate(out_chunks):
        wait_bytes(in1.at[path, :, :, pl.ds(start, size)], ring - 1, send1.at[n])
        for b in range(SLOTS):
            part = out2.at[b, path, :, :, pl.ds(start, size)]
            wait_bytes(part, blocks - 1, send2.at[b * chunks + n])
    for n, (path, start, size) in enumerate(back_chunks):
        wait_bytes(out4.at[path, :, :, pl.ds(start, size)], ring - 1, send4.at[n])
        for b in range(SLOTS):
            part = out3.at[b, path, :, :, pl.ds(start, size)]
            wait_bytes(part, blocks - 1, send3.at[b * chunks + n])


def shards(tokens, expert_ids, gate_weights, w_gate, w_up, w_down):
    toks, width = tokens.shape
    ff = w_gate.shape[2]
    ring = lax.axis_size("grp")
    blocks = lax.axis_size("exp")
    assert blocks == 2 * ring
    experts = ring * blocks
    rows1, rows2 = ring * toks, blocks * ring
    vmem = pl.BlockSpec(memory_space=pltpu.VMEM)
    hbm = pl.BlockSpec(memory_space=pl.ANY)
    wide = pltpu.VMEM((SLOTS, 2, blocks, ring, width // 2), BF16)
    narrow = pltpu.VMEM((2, ring, toks, width // 2), BF16)
    sems = pltpu.SemaphoreType.DMA((2 * len(CUTS) + 2,))
    more = pltpu.SemaphoreType.DMA((SLOTS * (2 * len(CUTS) + 2),))
    return pl.pallas_call(
        functools.partial(kernel, ring),
        out_shape=jax.ShapeDtypeStruct((toks, width), F32),
        in_specs=[hbm] * 6,
        out_specs=vmem,
        scratch_shapes=[
            pltpu.VMEM(expert_ids.shape[::-1], jnp.int32),
            pltpu.VMEM(expert_ids.shape[::-1], BF16),
            pltpu.VMEM((toks, width), BF16),
            pltpu.VMEM((toks, experts), BF16),
            pltpu.VMEM((2, ring, toks, experts), BF16),
            pltpu.VMEM((2, SLOTS, rows1, rows2), BF16),
            pltpu.VMEM((2, SLOTS, rows2, rows1), BF16),
            narrow, wide, wide, wide, wide, narrow, narrow,
            pltpu.VMEM((width, ff), BF16),
            pltpu.VMEM((width, ff), BF16),
            pltpu.VMEM((ff, width), BF16),
            pltpu.VMEM((rows2, ff), F32),
            pltpu.VMEM((rows2, ff), F32),
            pltpu.VMEM((2, rows2, ff), BF16),
            pltpu.VMEM((2, rows1, width // 2), F32),
            pltpu.SemaphoreType.DMA((3,)),
            pltpu.SemaphoreType.DMA((3,)),
            pltpu.SemaphoreType.DMA((2,)),
            pltpu.SemaphoreType.DMA((2,)),
            sems, sems, more, more, more, more, sems, sems,
        ],
        compiler_params=pltpu.CompilerParams(
            collective_id=0, has_side_effects=True, vmem_limit_bytes=VMEM_BYTES
        ),
    )(*(
        pltpu.with_memory_space_constraint(x, pltpu.HBM)
        for x in (expert_ids.T, gate_weights.T, tokens, w_gate[0], w_up[0], w_down[0])
    ))


def solution(mesh):
    return jax.shard_map(
        shards,
        mesh=mesh,
        in_specs=(
            P(("rep", "grp", "exp"), None),
            P(("rep", "grp", "exp"), None),
            P(("rep", "grp", "exp"), None),
            P(("grp", "exp"), None, None),
            P(("grp", "exp"), None, None),
            P(("grp", "exp"), None, None),
        ),
        out_specs=P(("rep", "grp", "exp"), None),
        check_vma=False,
    )
```

```python
import functools
import jax
import jax.numpy as jnp
from jax import lax
from jax.experimental import pallas as pl
from jax.experimental.pallas import tpu as pltpu
from jax.sharding import PartitionSpec as P

F32 = jnp.float32
BF16 = jnp.bfloat16
CUTS = (512,)
BACK = 1
SLOTS = 2
TILE = 256
VMEM_BYTES = 48 * 1024 * 1024


def iota(shape, dim):
    return lax.broadcasted_iota(jnp.int32, shape, dim)


def dot(a, b):
    return jnp.dot(a, b, preferred_element_type=F32)


def dot_nt(a, b):
    return lax.dot_general(a, b, (((1,), (1,)), ((), ())), preferred_element_type=F32)


def kernel(
    ring,
    ids_hbm, gates_hbm, tok_hbm, wg_hbm, wu_hbm, wd_hbm, o_ref,
    ids_ref, gates_ref, tok_ref, g_own, g_in, c_tab, s_tab, in1, out2, in2, out3, in3, out4, in4,
    wg, wu, wd, acc_g, acc_u, hid, sums,
    x_sem, w_sem, g_send, g_recv, send1, recv1, send2, recv2, send3, recv3, send4, recv4,
):
    toks, width = tok_hbm.shape
    ff = wg.shape[1]
    blocks = 2 * ring
    rows2 = blocks * ring
    rows1 = ring * toks
    experts = ring * blocks
    z = lax.axis_index("grp")
    e = lax.axis_index("exp")
    y = lax.div(e, 2)
    c = lax.rem(e, 2)

    half = width // 2
    edges = (0,) + CUTS + (half,)
    out_chunks = [
        (path, left, right - left) for left, right in zip(edges, edges[1:]) for path in range(2)
    ]
    back_chunks = [
        (path, left, size)
        for _, left, size in out_chunks[::2][::BACK] for path in range(2)
    ]
    chunks = len(out_chunks)

    order = [ring // 2 + ((j + 1) // 2) * (1 - 2 * (j % 2)) for j in range(ring - 1)]
    zs = {d: lax.rem(z + d, ring) for d in order}
    ys = {d: lax.rem(y + d, ring) * 2 for d in order}
    flip = 1 - c
    near_me = (z, y)
    far_me = (e, z * 2 + c)
    near = (
        [(zs[d], {"grp": zs[d], "exp": e}) for d in order],
        [(lax.div(ys[d], 2), {"grp": z, "exp": ys[d] + c}) for d in order],
    )
    far = (
        [(ys[d] + k, {"grp": z, "exp": ys[d] + k}) for d in order for k in (c, flip)]
        + [(y * 2 + flip, {"grp": z, "exp": y * 2 + flip})],
        [(zs[d] * 2 + k, {"grp": zs[d], "exp": y * 2 + k}) for d in order for k in (c, flip)]
        + [(z * 2 + flip, {"grp": z, "exp": y * 2 + flip})],
    )

    def remote(src, dst, send, recv, device):
        return pltpu.make_async_remote_copy(
            src_ref=src, dst_ref=dst, send_sem=send, recv_sem=recv,
            device_id=device, device_id_type=pl.DeviceIdType.MESH,
        )

    def wait_bytes(ref, count, sem):
        part = ref.at[pl.ds(0, count)]
        pltpu.make_async_copy(part, part, sem).wait()

    inputs = [
        pltpu.make_async_copy(hbm, vmem, x_sem.at[i])
        for i, (hbm, vmem) in enumerate(
            ((ids_hbm, ids_ref), (gates_hbm, gates_ref), (tok_hbm, tok_ref))
        )
    ]
    for copy in inputs:
        copy.start()

    barrier = pltpu.get_barrier_semaphore()

    for _, device in far[0] + far[1][:-1]:
        pl.semaphore_signal(
            barrier, inc=1, device_id=device, device_id_type=pl.DeviceIdType.MESH
        )

    inputs[0].wait()
    inputs[1].wait()
    table = jnp.zeros((experts, toks), F32)
    expert = iota((experts, toks), 0)
    for k in range(ids_ref.shape[0]):
        table = table + jnp.where(
            ids_ref[k:k + 1, :] == expert, gates_ref[k:k + 1, :].astype(F32), 0.0
        )
    same = jnp.where(iota((toks, toks), 0) == iota((toks, toks), 1), 1.0, 0.0).astype(BF16)
    table = dot_nt(same, table.astype(BF16)).astype(BF16)
    g_own[...] = table
    for path in range(2):
        g_in[path, near_me[path]] = table
    inputs[2].wait()

    pl.semaphore_wait(barrier, 4 * (ring - 1) + 1)

    for path in range(2):
        for _, device in near[path]:
            remote(
                g_own, g_in.at[path, near_me[path]], g_send.at[path], g_recv.at[path], device
            ).start()
    def block(path, source, start, size):
        return in1.at[path, source, :, pl.ds(start, size)]

    for n, (path, start, size) in enumerate(out_chunks):
        for _, device in near[path]:
            remote(
                tok_ref.at[:, pl.ds(path * half + start, size)],
                block(path, near_me[path], start, size),
                send1.at[n], recv1.at[n], device,
            ).start()

    loads = [
        pltpu.make_async_copy(hbm, vmem, w_sem.at[i])
        for i, (hbm, vmem) in enumerate(((wg_hbm, wg), (wu_hbm, wu), (wd_hbm, wd)))
    ]
    for load in loads:
        load.start()
    for path in range(2):
        in1[path, near_me[path]] = tok_ref[:, path * half:(path + 1) * half]

    def expert_of(path, place):
        block = place // ring
        if path == 0:
            return z * blocks + block
        return (block // 2) * blocks + y * 2 + lax.rem(block, 2)

    ranks = []
    for path in range(2):
        wait_bytes(g_in.at[path], ring - 1, g_recv.at[path])
        gates = g_in[path].reshape(rows1, experts)
        named = jnp.where(gates.astype(F32) > 0, 1.0, 0.0).astype(BF16)
        r, q = iota((rows1, rows1), 0), iota((rows1, rows1), 1)
        below = jnp.where((r // toks == q // toks) & (q < r), 1.0, 0.0).astype(BF16)
        rank = dot(below, named).astype(BF16)
        ranks.append(rank)
        pick = jnp.where(
            iota((rows2, experts), 1) == expert_of(path, iota((rows2, experts), 0)), 1.0, 0.0
        ).astype(BF16)
        own = iota((rows2, rows1), 1) // toks == lax.rem(iota((rows2, rows1), 0), ring)
        own = own & (dot_nt(pick, gates) > 0)
        place = dot_nt(pick, rank)
        for b in range(SLOTS):
            s_tab[path, b] = jnp.where(own & (place == b), 1.0, 0.0).astype(BF16)

    for b in range(SLOTS):
        for i, (path, start, size) in enumerate(out_chunks):
            n = b * chunks + i
            at = slice(start, start + size)
            if b == 0:
                wait_bytes(in1.at[path, :, :, pl.ds(start, size)], ring - 1, recv1.at[i])
            rows = in1[path, :, :, at].reshape(rows1, size)
            chosen = dot(s_tab[path, b], rows).astype(BF16)
            out2[b, path, :, :, at] = chosen.reshape(blocks, ring, size)
            in2[b, path, far_me[path], :, at] = out2[b, path, far_me[path], :, at]
            for to, device in far[path]:
                remote(
                    out2.at[b, path, to, :, pl.ds(start, size)],
                    in2.at[b, path, far_me[path], :, pl.ds(start, size)],
                    send2.at[n], recv2.at[n], device,
                ).start()

    for path in range(2):
        gates = g_in[path].reshape(rows1, experts)
        rank = ranks[path]
        pick = jnp.where(
            iota((experts, rows2), 0) == expert_of(path, iota((experts, rows2), 1)), 1.0, 0.0
        ).astype(BF16)
        own = iota((rows1, rows2), 0) // toks == lax.rem(iota((rows1, rows2), 1), ring)
        value, place = dot(gates, pick), dot(rank, pick)
        for b in range(SLOTS):
            c_tab[path, b] = jnp.where(own & (place == b), value, 0.0).astype(BF16)

    r, q = iota((rows2, rows2), 0), iota((rows2, rows2), 1)
    swapped = (
        lax.rem(r, ring) * blocks + lax.rem(r // ring, 2) * ring + r // blocks
    )
    swap = jnp.where(q == swapped, 1.0, 0.0).astype(BF16)

    for b in range(SLOTS):
        last = len(out_chunks) - 1
        for i, (path, start, size) in enumerate(out_chunks):
            n = b * chunks + i
            wait_bytes(in2.at[b, path, :, :, pl.ds(start, size)], blocks - 1, recv2.at[n])
            rows = in2[b, path, :, :, start:start + size].reshape(rows2, size)
            if path == 1:
                rows = dot(swap, rows).astype(BF16)
            if n == 0:
                loads[0].wait()
                loads[1].wait()

            def project(j, x, i=i, rows=rows, top=path * half + start, size=size, last=last):
                at = pl.ds(pl.multiple_of(j * TILE, TILE), TILE)
                gate_part = dot(rows, wg[top:top + size, at])
                up_part = dot(rows, wu[top:top + size, at])
                if i > 0:
                    gate_part = gate_part + acc_g[:, at]
                    up_part = up_part + acc_u[:, at]
                if i < last:
                    acc_g[:, at] = gate_part
                    acc_u[:, at] = up_part
                else:
                    hid[0, :, at] = (
                        gate_part * jax.nn.sigmoid(gate_part) * up_part
                    ).astype(BF16)
                return x
            lax.fori_loop(0, ff // TILE, project, 0)
        hid[1] = dot(swap, hid[0]).astype(BF16)
        if b == 0:
            loads[2].wait()

        for i, (path, start, size) in enumerate(back_chunks):
            n = b * chunks + i
            hidden = hid[path]

            def down(j, x, b=b, path=path, start=start, hidden=hidden):
                at = pl.ds(pl.multiple_of(start + j * TILE, TILE), TILE)
                here = pl.ds(pl.multiple_of(path * half + start + j * TILE, TILE), TILE)
                out3[b, path, :, :, at] = dot(hidden, wd[:, here]).astype(BF16).reshape(
                    blocks, ring, TILE
                )
                return x
            lax.fori_loop(0, size // TILE, down, 0)
            at = slice(start, start + size)
            in3[b, path, far_me[path], :, at] = out3[b, path, far_me[path], :, at]
            for to, device in far[path]:
                remote(
                    out3.at[b, path, to, :, pl.ds(start, size)],
                    in3.at[b, path, far_me[path], :, pl.ds(start, size)],
                    send3.at[n], recv3.at[n], device,
                ).start()

    def weigh(b, n, path, start, size):
        part = in3.at[b, path, :, :, pl.ds(start, size)]
        wait_bytes(part, blocks - 1, recv3.at[b * chunks + n])
        back = in3[b, path, :, :, start:start + size].reshape(rows2, size)
        return dot(c_tab[path, b], back)

    for n, (path, start, size) in enumerate(back_chunks):
        sums[path, :, start:start + size] = weigh(0, n, path, start, size)
    for n, (path, start, size) in enumerate(back_chunks):
        at = slice(start, start + size)
        summed = sums[path, :, at] + weigh(1, n, path, start, size)
        out4[path, :, :, at] = summed.astype(BF16).reshape(ring, toks, size)
        in4[path, near_me[path], :, at] = out4[path, near_me[path], :, at]
        for to, device in near[path]:
            remote(
                out4.at[path, to, :, pl.ds(start, size)],
                in4.at[path, near_me[path], :, pl.ds(start, size)],
                send4.at[n], recv4.at[n], device,
            ).start()

    for n, (path, start, size) in enumerate(back_chunks):
        wait_bytes(in4.at[path, :, :, pl.ds(start, size)], ring - 1, recv4.at[n])
        at = slice(start, start + size)
        total = in4[path, 0, :, at].astype(F32)
        for i in range(1, ring):
            total = total + in4[path, i, :, at].astype(F32)
        o_ref[:, path * half + start:path * half + start + size] = total

    for path in range(2):
        wait_bytes(g_in.at[path], ring - 1, g_send.at[path])
    for n, (path, start, size) in enumerate(out_chunks):
        wait_bytes(in1.at[path, :, :, pl.ds(start, size)], ring - 1, send1.at[n])
        for b in range(SLOTS):
            part = out2.at[b, path, :, :, pl.ds(start, size)]
            wait_bytes(part, blocks - 1, send2.at[b * chunks + n])
    for n, (path, start, size) in enumerate(back_chunks):
        wait_bytes(out4.at[path, :, :, pl.ds(start, size)], ring - 1, send4.at[n])
        for b in range(SLOTS):
            part = out3.at[b, path, :, :, pl.ds(start, size)]
            wait_bytes(part, blocks - 1, send3.at[b * chunks + n])


def shards(tokens, expert_ids, gate_weights, w_gate, w_up, w_down):
    toks, width = tokens.shape
    ff = w_gate.shape[2]
    ring = lax.axis_size("grp")
    blocks = lax.axis_size("exp")
    assert blocks == 2 * ring
    experts = ring * blocks
    rows1, rows2 = ring * toks, blocks * ring
    vmem = pl.BlockSpec(memory_space=pltpu.VMEM)
    hbm = pl.BlockSpec(memory_space=pl.ANY)
    wide = pltpu.VMEM((SLOTS, 2, blocks, ring, width // 2), BF16)
    narrow = pltpu.VMEM((2, ring, toks, width // 2), BF16)
    sems = pltpu.SemaphoreType.DMA((2 * len(CUTS) + 2,))
    more = pltpu.SemaphoreType.DMA((SLOTS * (2 * len(CUTS) + 2),))
    return pl.pallas_call(
        functools.partial(kernel, ring),
        out_shape=jax.ShapeDtypeStruct((toks, width), F32),
        in_specs=[hbm] * 6,
        out_specs=vmem,
        scratch_shapes=[
            pltpu.VMEM(expert_ids.shape[::-1], jnp.int32),
            pltpu.VMEM(expert_ids.shape[::-1], BF16),
            pltpu.VMEM((toks, width), BF16),
            pltpu.VMEM((toks, experts), BF16),
            pltpu.VMEM((2, ring, toks, experts), BF16),
            pltpu.VMEM((2, SLOTS, rows1, rows2), BF16),
            pltpu.VMEM((2, SLOTS, rows2, rows1), BF16),
            narrow, wide, wide, wide, wide, narrow, narrow,
            pltpu.VMEM((width, ff), BF16),
            pltpu.VMEM((width, ff), BF16),
            pltpu.VMEM((ff, width), BF16),
            pltpu.VMEM((rows2, ff), F32),
            pltpu.VMEM((rows2, ff), F32),
            pltpu.VMEM((2, rows2, ff), BF16),
            pltpu.VMEM((2, rows1, width // 2), F32),
            pltpu.SemaphoreType.DMA((3,)),
            pltpu.SemaphoreType.DMA((3,)),
            pltpu.SemaphoreType.DMA((2,)),
            pltpu.SemaphoreType.DMA((2,)),
            sems, sems, more, more, more, more, sems, sems,
        ],
        compiler_params=pltpu.CompilerParams(
            collective_id=0, has_side_effects=True, vmem_limit_bytes=VMEM_BYTES
        ),
    )(*(
        pltpu.with_memory_space_constraint(x, pltpu.HBM)
        for x in (expert_ids.T, gate_weights.T, tokens, w_gate[0], w_up[0], w_down[0])
    ))


def solution(mesh):
    return jax.shard_map(
        shards,
        mesh=mesh,
        in_specs=(
            P(("rep", "grp", "exp"), None),
            P(("rep", "grp", "exp"), None),
            P(("rep", "grp", "exp"), None),
            P(("grp", "exp"), None, None),
            P(("grp", "exp"), None, None),
            P(("grp", "exp"), None, None),
        ),
        out_specs=P(("rep", "grp", "exp"), None),
        check_vma=False,
    )
```
